32 devices in a mesh: narrow: 2 (over y), wide: 16 (over z, x, core).
Axes of the slice: x: 2, y: 2, z: 4, core: 2. Of those that a mesh axis runs over, the one named last changes fastest.
Arguments:
- u_real: bfloat16 [1024, 131072], P('narrow', 'wide'), may hold values from -0.01171875 to 0.01171875
- u_imag: bfloat16 [1024, 131072], P('narrow', 'wide'), may hold values from -0.01171875 to 0.01171875
- psi_real: bfloat16 [131072, 512], P('wide', 'narrow'), may hold values from -6 to 6
- psi_imag: bfloat16 [131072, 512], P('wide', 'narrow'), may hold values from -6 to 6
- kick_angle: float32 [512], P('narrow'), may hold values from 0.3 to 2.5
- excited: int32 [131072], P('wide'), may hold values from 0 to 12
Outputs:
- out_real: float32 [512, 1024], P('wide', 'narrow')
- out_imag: float32 [512, 1024], P('wide', 'narrow')
The draws below stay inside these ranges and needn't reach their ends.
All inputs are finite; a program needn't handle non-finite values.
Results may differ from the reference program's by a relative error of at most 0.0028.
Values may be sent and summed in bfloat16 or wider, within the bound.
No kernel may reach another device: no remote copies, remote signals or barrier semaphores. Data moves between devices by JAX's collectives and lax.ppermute only.
A program may use at most 128 MiB of HBM per device.

```python
import math
import jax
import jax.numpy as jnp
from jax import lax

DIM = 131072
ROWS = 1024
STATES = 512
MOST_EXCITED = 12


def with_ends(array, rng, least, largest):
    extent = array.shape
    place = [jax.random.randint(jax.random.fold_in(rng, axis), (), 0, extent[axis]) for axis in range(len(extent))]
    array = array.at[tuple(place)].set(least)
    longest = extent.index(max(extent))
    place[longest] = (place[longest] + 1) % extent[longest]
    return array.at[tuple(place)].set(largest)


def steps_of(key, extent, cuts, low, high):
    level = 1.0
    for axis_at, parts in cuts:
        heights = jax.random.uniform(jax.random.fold_in(jax.random.fold_in(key, 6), axis_at), (parts,), jnp.float32, low / len(cuts), high / len(cuts))
        level = level * jnp.repeat(jnp.exp(heights), extent[axis_at] // parts).reshape((-1,) + (1,) * (len(extent) - 1 - axis_at))
    return level


def bell_draw(stream_key, dims, spread, reach, cuts=(), dtype=jnp.bfloat16):
    array = spread * jax.random.normal(stream_key, dims, jnp.float32)
    if cuts:
        array = array * steps_of(stream_key, dims, cuts, -0.22, 0.18)
    return jnp.clip(array, -reach, reach).astype(dtype)


def setup_inputs(seed: int = 0) -> dict:
    key_list = jax.random.split(jax.random.key(seed), 7)
    u_real = bell_draw(key_list[0], (ROWS, DIM), (2 * DIM) ** -0.5, 0.01171875, ((0, 2), (1, 16)))
    u_imag = bell_draw(key_list[1], (ROWS, DIM), (2 * DIM) ** -0.5, 0.01171875, ((0, 2), (1, 16)))
    psi_real = bell_draw(key_list[2], (DIM, STATES), 1.0, 6.0, ((0, 16), (1, 2)))
    psi_imag = bell_draw(key_list[3], (DIM, STATES), 1.0, 6.0, ((0, 16), (1, 2)))
    kick_angle = jnp.clip(jnp.exp(math.log(2.5) - 2.1202635 * jax.random.uniform(key_list[4], (STATES,), jnp.float32) ** steps_of(key_list[4], (STATES,), ((0, 2),), -0.2, 0.2)), 0.3, 2.5)
    excited = with_ends(jax.random.randint(key_list[5], (DIM,), 0, MOST_EXCITED + 1), jax.random.fold_in(key_list[5], 1), 0, MOST_EXCITED).astype(jnp.int32)
    return {"u_real": u_real, "u_imag": u_imag, "psi_real": psi_real, "psi_imag": psi_imag, "kick_angle": kick_angle, "excited": excited}


def apply_kick(psi_real, psi_imag, kick_angle, excited):
    phases = excited.astype(jnp.float32)[:, None] * kick_angle[None, :]
    cosine = jnp.cos(phases)
    sine = jnp.sin(phases)
    part_real = psi_real.astype(jnp.float32)
    part_imag = psi_imag.astype(jnp.float32)
    kicked_real = (cosine * part_real + sine * part_imag).astype(jnp.bfloat16)
    kicked_imag = (cosine * part_imag - sine * part_real).astype(jnp.bfloat16)
    return kicked_real, kicked_imag


def reference(u_real, u_imag, psi_real, psi_imag, kick_angle, excited):
    span_cols = min(DIM, 8192)
    blocks = DIM // span_cols
    contract = (((0,), (1,)), ((), ()))

    def step(position, totals):
        first_col = (position * span_cols).astype(jnp.int32)
        rows_real = lax.dynamic_slice_in_dim(u_real, first_col, span_cols, 1)
        rows_imag = lax.dynamic_slice_in_dim(u_imag, first_col, span_cols, 1)
        block_real = lax.dynamic_slice_in_dim(psi_real, first_col, span_cols, 0)
        block_imag = lax.dynamic_slice_in_dim(psi_imag, first_col, span_cols, 0)
        block_excited = lax.dynamic_slice_in_dim(excited, first_col, span_cols, 0)
        kicked_real, kicked_imag = apply_kick(block_real, block_imag, kick_angle, block_excited)
        rr = lax.dot_general(kicked_real, rows_real, contract, preferred_element_type=jnp.float32)
        ii = lax.dot_general(kicked_imag, rows_imag, contract, preferred_element_type=jnp.float32)
        ri = lax.dot_general(kicked_imag, rows_real, contract, preferred_element_type=jnp.float32)
        ir = lax.dot_general(kicked_real, rows_imag, contract, preferred_element_type=jnp.float32)
        return (totals[0] + rr - ii, totals[1] + ri + ir)

    empty = jnp.zeros((STATES, ROWS), jnp.float32)
    out_real, out_imag = lax.fori_loop(0, blocks, step, (empty, empty))
    return out_real, out_imag
```

```python
import functools

import jax
import jax.numpy as jnp
from jax import lax
from jax.experimental import pallas as pl
from jax.experimental.pallas import tpu as pltpu
from jax.sharding import PartitionSpec as P

LEVELS = 16


def bits_of(n):
    return n.bit_length() - 1


def parts_of(value):
    high = lax.reduce_precision(value, 8, 7)
    rest = value - high
    middle = lax.reduce_precision(rest, 8, 7)
    return jnp.concatenate([high, middle, rest - middle], axis=1).astype(jnp.bfloat16)


def kick_kernel(owners, each, first, count, table_ref, excited_ref, real_ref, imag_ref, out_ref):
    size = owners * count
    level = lax.broadcasted_iota(jnp.int32, (LEVELS, excited_ref.shape[1]), 0)
    hot = jnp.where(level == excited_ref[...], 1.0, 0.0)
    hot = jnp.concatenate([hot, hot, hot], axis=0).astype(jnp.bfloat16)
    waves = jnp.dot(table_ref[...], hot, preferred_element_type=jnp.float32)
    cosine, sine = waves[:size], waves[size:]

    def rows(ref):
        block = ref[...].astype(jnp.float32).T
        return jnp.concatenate(
            [block[o * each + first : o * each + first + count] for o in range(owners)], axis=0
        )

    real, imag = rows(real_ref), rows(imag_ref)
    out_ref[:size, :] = (cosine * real + sine * imag).astype(jnp.bfloat16)
    out_ref[size:, :] = (cosine * imag - sine * real).astype(jnp.bfloat16)


def kick(owners, each, first, count, start, length, table, excited, real, imag):
    depth, states = real.shape
    block = min(1024, length)
    offset = start // block
    size = owners * count
    return pl.pallas_call(
        functools.partial(kick_kernel, owners, each, first, count),
        grid=(length // block,),
        out_shape=jax.ShapeDtypeStruct((2 * size, length), jnp.bfloat16),
        in_specs=[
            pl.BlockSpec(table.shape, lambda i: (0, 0)),
            pl.BlockSpec((1, block), lambda i: (0, i + offset)),
            pl.BlockSpec((block, states), lambda i: (i + offset, 0)),
            pl.BlockSpec((block, states), lambda i: (i + offset, 0)),
        ],
        out_specs=pl.BlockSpec((2 * size, block), lambda i: (0, i)),
        cost_estimate=pl.CostEstimate(
            flops=8 * size * length, bytes_accessed=4 * length * (states + size), transcendentals=0
        ),
        name="kick",
    )(table, excited, real, imag)


def multiply_kernel(owners, count, steps, has_total, place_ref, states_ref, real_ref, imag_ref, *refs):
    if has_total:
        total_ref, out_ref, sum_ref = refs
    else:
        out_ref, sum_ref = refs
    size = owners * count
    local_rows = real_ref.shape[0]
    contract = (((1,), (1,)), ((), ()))
    step = pl.program_id(0)
    by_real = lax.dot_general(states_ref[...], real_ref[...], contract, preferred_element_type=jnp.float32)
    by_imag = lax.dot_general(states_ref[...], imag_ref[...], contract, preferred_element_type=jnp.float32)
    part_real = by_real[:size] - by_imag[size:]
    part_imag = by_real[size:] + by_imag[:size]

    @pl.when(step == 0)
    def _():
        sum_ref[:, :local_rows] = part_real
        sum_ref[:, local_rows:] = part_imag

    @pl.when(step > 0)
    def _():
        sum_ref[:, :local_rows] += part_real
        sum_ref[:, local_rows:] += part_imag

    @pl.when(step == steps - 1)
    def _():
        for o in range(owners):
            to = pl.multiple_of(place_ref[o] * count, 8)
            piece = sum_ref[o * count : (o + 1) * count, :]
            if has_total:
                piece = piece + total_ref[pl.ds(to, count), :]
            out_ref[pl.ds(to, count), :] = piece


def multiply(owners, count, start, place, states, u_real, u_imag, total):
    length = states.shape[1]
    local_rows = u_real.shape[0]
    size = owners * count
    block = min(1024, length)
    steps = length // block
    offset = start // block
    whole = pl.BlockSpec((size, 2 * local_rows), lambda i: (0, 0))
    in_specs = [
        pl.BlockSpec(memory_space=pltpu.SMEM),
        pl.BlockSpec((2 * size, block), lambda i: (0, i)),
        pl.BlockSpec((local_rows, block), lambda i: (0, i + offset)),
        pl.BlockSpec((local_rows, block), lambda i: (0, i + offset)),
    ]
    args = [place, states, u_real, u_imag]
    if total is not None:
        in_specs.append(whole)
        args.append(total)
    return pl.pallas_call(
        functools.partial(multiply_kernel, owners, count, steps, total is not None),
        grid=(steps,),
        out_shape=jax.ShapeDtypeStruct((size, 2 * local_rows), jnp.float32),
        in_specs=in_specs,
        out_specs=whole,
        scratch_shapes=[pltpu.VMEM((size, 2 * local_rows), jnp.float32)],
        cost_estimate=pl.CostEstimate(
            flops=8 * size * local_rows * length,
            bytes_accessed=4 * length * (local_rows + size) + 8 * size * local_rows,
            transcendentals=0,
        ),
        name="multiply",
    )(*args)


def solution(mesh):
    narrow, wide = mesh.shape["narrow"], mesh.shape["wide"]
    owners = wide // narrow
    low, high = bits_of(owners), bits_of(narrow)
    both = ("narrow", "wide")

    def swap(bit):
        return [(w, w ^ bit) for w in range(wide)]

    def scatter(value, source):
        for b in range(low):
            half = value.shape[0] // 2
            value = value[:half] + lax.ppermute(value[half:], "wide", swap(1 << b))
        for b in range(high):
            pairs = []
            for n in range(narrow):
                for w in range(wide):
                    to = w ^ (owners << b)
                    if (((w // owners) ^ n ^ source) >> b) & 1:
                        pairs.append((n * wide + w, n * wide + to))
            value = value + lax.ppermute(value, both, pairs)
        return value

    def on_device(u_real, u_imag, psi_real, psi_imag, kick_angle, excited):
        local_rows, depth = u_real.shape
        states = psi_real.shape[1]
        each = states // owners
        groups = [(0, each - 8), (each - 8, 8)] if each > 8 else [(0, each)]
        n = lax.axis_index("narrow")
        w = lax.axis_index("wide")
        mine = lax.rem(w, owners)
        place = jnp.arange(owners, dtype=jnp.int32) ^ mine
        place = sum((((place >> b) & 1) << (low - 1 - b) for b in range(low)), jnp.zeros((owners,), jnp.int32))
        top = w // owners

        phases = kick_angle[:, None] * jnp.arange(LEVELS, dtype=jnp.float32)[None, :]
        cosine = parts_of(jnp.cos(phases)).reshape(owners, each, 3 * LEVELS)
        sine = parts_of(jnp.sin(phases)).reshape(owners, each, 3 * LEVELS)
        excited = excited.reshape(1, depth)

        unit = depth // 8
        cuts = {0: [1, 1, 2, 4], len(groups) - 1: [4, 3, 1]}
        if len(groups) == 1:
            cuts = {0: [1, 1, 2, 2, 1, 1]}
        pieces = []
        for g, (first, count) in enumerate(groups):
            table = jnp.concatenate(
                [t[:, first : first + count].reshape(owners * count, 3 * LEVELS) for t in (cosine, sine)], axis=0
            )
            start = 0
            mine_of_group = []
            for cut in cuts[g]:
                length = cut * unit
                piece = kick(owners, each, first, count, start, length, table, excited, psi_real, psi_imag)
                mine_of_group.append((start, piece))
                start += length
            pieces.append(mine_of_group)

        arrived = {}
        for source in range(1, narrow):
            pairs = [(a, a ^ source) for a in range(narrow)]
            for g in range(len(groups)):
                arrived[source, g] = [(start, lax.ppermute(piece, "narrow", pairs)) for start, piece in pieces[g]]

        out = None
        for source in range(narrow):
            blocks = []
            for g, (first, count) in enumerate(groups):
                total = None
                for start, piece in pieces[g] if source == 0 else arrived[source, g]:
                    total = multiply(owners, count, start, place, piece, u_real, u_imag, total)
                blocks.append(scatter(total, source))
            block = jnp.concatenate(blocks, axis=0)
            out = block if out is None else jnp.where(top == (n ^ source), block, out)
        return out[:, :local_rows], out[:, local_rows:]

    in_specs = (
        P("narrow", "wide"),
        P("narrow", "wide"),
        P("wide", "narrow"),
        P("wide", "narrow"),
        P("narrow"),
        P("wide"),
    )
    out_specs = (P("wide", "narrow"), P("wide", "narrow"))
    return jax.shard_map(on_device, mesh=mesh, in_specs=in_specs, out_specs=out_specs, check_vma=False)
```

```python
import functools

import jax
import jax.numpy as jnp
from jax import lax
from jax.experimental import pallas as pl
from jax.experimental.pallas import tpu as pltpu
from jax.sharding import PartitionSpec as P

LEVELS = 16
CONTRACT = (((1,), (1,)), ((), ()))
MIB = 1 << 20


def bits_of(n):
    return n.bit_length() - 1


def parts_of(value):
    high = lax.reduce_precision(value, 8, 7)
    rest = value - high
    middle = lax.reduce_precision(rest, 8, 7)
    return jnp.concatenate([high, middle, rest - middle], axis=1).astype(jnp.bfloat16)


def table_of(kick_angle):
    phases = kick_angle[:, None] * jnp.arange(LEVELS, dtype=jnp.float32)[None, :]
    return jnp.concatenate([parts_of(jnp.cos(phases)), parts_of(jnp.sin(phases))], axis=0)


def kicked(table_ref, excited_ref, real_ref, imag_ref):
    states = real_ref.shape[1]
    level = lax.broadcasted_iota(jnp.int32, (LEVELS, excited_ref.shape[1]), 0)
    hot = jnp.where(level == excited_ref[...], 1.0, 0.0)
    hot = jnp.concatenate([hot, hot, hot], axis=0).astype(jnp.bfloat16)
    waves = jnp.dot(table_ref[...], hot, preferred_element_type=jnp.float32)
    cosine, sine = waves[:states], waves[states:]
    real, imag = real_ref[...].astype(jnp.float32).T, imag_ref[...].astype(jnp.float32).T
    return cosine * real + sine * imag, cosine * imag - sine * real


def kick_kernel(owners, each, groups, table_ref, excited_ref, real_ref, imag_ref, *out_refs):
    parts = kicked(table_ref, excited_ref, real_ref, imag_ref)
    for (first, count), out_ref in zip(groups, out_refs):
        size = owners * count
        for at, part in enumerate(parts):
            rows = [part[o * each + first : o * each + first + count] for o in range(owners)]
            out_ref[at * size : (at + 1) * size, :] = jnp.concatenate(rows, axis=0).astype(jnp.bfloat16)


def kick_placed_kernel(owners, each, place_ref, table_ref, excited_ref, real_ref, imag_ref, out_ref):
    real, imag = kicked(table_ref, excited_ref, real_ref, imag_ref)
    for o in range(owners):
        rows = slice(o * each, (o + 1) * each)
        to = pl.multiple_of(place_ref[o] * (2 * each), 2 * each)
        out_ref[pl.ds(to, 2 * each), :] = jnp.concatenate([real[rows], imag[rows]], axis=0).astype(jnp.bfloat16)


def kick(owners, each, groups, block, start, length, table, excited, real, imag, skip=True, place=None):
    states = real.shape[1]
    offset = start // block
    inner = offset if skip else 0
    in_specs = [
        pl.BlockSpec(table.shape, lambda i: (0, 0)),
        pl.BlockSpec((1, block), lambda i: (0, i + offset)),
        pl.BlockSpec((block, states), lambda i: (i + inner, 0)),
        pl.BlockSpec((block, states), lambda i: (i + inner, 0)),
    ]
    args = [table, excited, real, imag]
    if place is None:
        kernel = functools.partial(kick_kernel, owners, each, groups)
        sizes = [2 * owners * count for _, count in groups]
    else:
        kernel = functools.partial(kick_placed_kernel, owners, each)
        sizes = [2 * states]
        in_specs.insert(0, pl.BlockSpec(memory_space=pltpu.SMEM))
        args.insert(0, place)
    return pl.pallas_call(
        kernel,
        grid=(length // block,),
        out_shape=[jax.ShapeDtypeStruct((size, length), jnp.bfloat16) for size in sizes],
        in_specs=in_specs,
        out_specs=[pl.BlockSpec((size, block), lambda i: (0, i)) for size in sizes],
        compiler_params=pltpu.CompilerParams(vmem_limit_bytes=24 * MIB),
        cost_estimate=pl.CostEstimate(flops=8 * states * length, bytes_accessed=8 * length * states, transcendentals=0),
        name="kick",
    )(*args)


def multiply_kernel(owners, counts, steps, has_total, split, place_ref, *refs):
    state_refs, refs = refs[: len(counts)], refs[len(counts) :]
    real_ref, imag_ref, refs = refs[0], refs[1], refs[2:]
    out_refs, sum_ref = refs[int(has_total) : -1], refs[-1]
    local_rows = real_ref.shape[0]
    step = pl.program_id(0)
    row = 0
    for count, states_ref in zip(counts, state_refs):
        size = owners * count
        by_real = lax.dot_general(states_ref[...], real_ref[...], CONTRACT, preferred_element_type=jnp.float32)
        by_imag = lax.dot_general(states_ref[...], imag_ref[...], CONTRACT, preferred_element_type=jnp.float32)
        part_real = by_real[:size] - by_imag[size:]
        part_imag = by_real[size:] + by_imag[:size]
        rows = slice(row, row + size)

        @pl.when(step == 0)
        def _():
            sum_ref[rows, :local_rows] = part_real
            sum_ref[rows, local_rows:] = part_imag

        @pl.when(step > 0)
        def _():
            sum_ref[rows, :local_rows] += part_real
            sum_ref[rows, local_rows:] += part_imag

        row += size

    def store(out_refs, piece, to):
        count, half = piece.shape[0], out_refs[0].shape[0]
        if not split:
            out_refs[0][pl.ds(to, count), :] = piece
            return

        @pl.when(to < half)
        def _():
            out_refs[0][pl.ds(to, count), :] = piece

        @pl.when(to >= half)
        def _():
            out_refs[1][pl.ds(pl.multiple_of(to - half, 8), count), :] = piece

    @pl.when(step == steps - 1)
    def _():
        for o in range(owners):
            row, to = 0, pl.multiple_of(place_ref[o] * sum(counts), 8)
            for count in counts:
                piece = sum_ref[row + o * count : row + (o + 1) * count, :]
                if has_total:
                    piece = piece + refs[0][pl.ds(to, count), :]
                store(out_refs, piece, to)
                row += owners * count
                to = pl.multiple_of(to + count, 8)


def multiply(owners, counts, block, start, place, states, u_real, u_imag, total, split=False):
    length = states[0].shape[1]
    local_rows = u_real.shape[0]
    size = owners * sum(counts)
    steps = length // block
    offset = start // block
    whole = pl.BlockSpec((size, 2 * local_rows), lambda i: (0, 0))
    in_specs = [pl.BlockSpec(memory_space=pltpu.SMEM)]
    in_specs += [pl.BlockSpec((2 * owners * count, block), lambda i: (0, i)) for count in counts]
    in_specs += [pl.BlockSpec((local_rows, block), lambda i: (0, i + offset))] * 2
    args = [place, *states, u_real, u_imag]
    if total is not None:
        in_specs.append(whole)
        args.append(total)
    results = pl.pallas_call(
        functools.partial(multiply_kernel, owners, counts, steps, total is not None, split),
        grid=(steps,),
        out_shape=[jax.ShapeDtypeStruct((size >> split, 2 * local_rows), jnp.float32)] * (1 + split),
        in_specs=in_specs,
        out_specs=[pl.BlockSpec((size >> split, 2 * local_rows), lambda i: (0, 0))] * (1 + split),
        scratch_shapes=[pltpu.VMEM((size, 2 * local_rows), jnp.float32)],
        compiler_params=pltpu.CompilerParams(vmem_limit_bytes=20 * MIB),
        cost_estimate=pl.CostEstimate(
            flops=8 * size * local_rows * length,
            bytes_accessed=4 * length * (local_rows + size) + 8 * size * local_rows,
            transcendentals=0,
        ),
        name="multiply",
    )(*args)
    return results if split else results[0]


def finish_kernel(each, pieces, has_total, held, states_ref, *refs):
    u_refs, out_ref = refs[:pieces], refs[-1]
    local_rows = u_refs[0].shape[0] // 2
    total = None
    for j in range(pieces):
        states = states_ref[2 * each * j : 2 * each * (j + 1), :]
        part = lax.dot_general(states, u_refs[j][...], CONTRACT, preferred_element_type=jnp.float32)
        total = part if total is None else total + part
    real = total[:each, :local_rows] - total[each:, local_rows:]
    imag = total[each:, :local_rows] + total[:each, local_rows:]
    if has_total:
        real = real + refs[pieces][:, :local_rows]
        imag = imag + refs[pieces][:, local_rows:]
    out_ref[:, :local_rows] = real
    out_ref[:, local_rows:] = imag
    for value_ref in refs[len(refs) - 1 - held : -1]:
        out_ref[each - value_ref.shape[0] :, :] += value_ref[...]


def finish(each, states, u_pieces, total, held):
    rows, length = u_pieces[0].shape
    args = [states, *u_pieces] + ([] if total is None else [total]) + held
    return pl.pallas_call(
        functools.partial(finish_kernel, each, len(u_pieces), total is not None, len(held)),
        out_shape=jax.ShapeDtypeStruct((each, rows), jnp.float32),
        compiler_params=pltpu.CompilerParams(vmem_limit_bytes=12 * MIB),
        cost_estimate=pl.CostEstimate(
            flops=4 * each * rows * length * len(u_pieces),
            bytes_accessed=2 * length * (rows + 2 * each) * len(u_pieces),
            transcendentals=0,
        ),
        name="finish",
    )(*args)


def combine_kernel(terms, flag_ref, *refs):
    real_ref, imag_ref = refs[-2:]
    _, local_rows = real_ref.shape
    for at, out_ref in enumerate((real_ref, imag_ref)):
        columns = slice(at * local_rows, (at + 1) * local_rows)
        sums = {}
        for (which, first), ref in zip(terms, refs):
            for key in ((which, first, ref.shape[0]),):
                value = ref[:, columns].astype(jnp.float32)
                sums[key] = sums[key] + value if key in sums else value
        out_ref[...] = jnp.zeros_like(out_ref)
        for (which, first, count), value in sums.items():
            out_ref[first : first + count, :] += jnp.where(flag_ref[which] > 0, value, 0.0)


def combine(flags, terms, rows, local_rows):
    shape = jax.ShapeDtypeStruct((rows, local_rows), jnp.float32)
    return pl.pallas_call(
        functools.partial(combine_kernel, [(which, first) for which, first, _ in terms]),
        out_shape=(shape, shape),
        in_specs=[pl.BlockSpec(memory_space=pltpu.SMEM)] + [pl.BlockSpec(memory_space=pltpu.VMEM)] * len(terms),
        compiler_params=pltpu.CompilerParams(vmem_limit_bytes=12 * MIB),
        name="combine",
    )(flags, *(value for _, _, value in terms))


def solution(mesh):
    narrow, wide = mesh.shape["narrow"], mesh.shape["wide"]
    owners = wide // narrow
    low, high = bits_of(owners), bits_of(narrow)
    both = ("narrow", "wide")

    def across(value, bit):
        return lax.ppermute(value, "wide", [(w, w ^ bit) for w in range(wide)])

    def scatter_low(value):
        keep, send = value
        for b in range(low):
            value = keep + across(send, 1 << b)
            half = value.shape[0] // 2
            keep, send = value[:half], value[half:]
        return value

    def hop_high(value, source, b, dtype=jnp.bfloat16):
        pairs = [
            (n * wide + w, n * wide + (w ^ (owners << b)))
            for n in range(narrow)
            for w in range(wide)
            if (((w // owners) ^ n ^ source) >> b) & 1
        ]
        return lax.ppermute(value.astype(dtype), both, pairs)

    def scatter_high(value, source, dtype=jnp.float32):
        *before, bit = range(high)
        for b in before:
            value = value + hop_high(value, source, b, dtype)
        return value, hop_high(value, source, bit, dtype)

    def on_device(u_real, u_imag, psi_real, psi_imag, kick_angle, excited):
        local_rows, depth = u_real.shape
        states = psi_real.shape[1]
        each = states // owners
        unit = depth // 16
        groups = [(0, each - 8), (each - 8, 8)] if each > 8 else [(0, each)]
        counts = [count for _, count in groups]
        raw, last = 2 * unit, depth - unit
        cuts = [(raw, 5 * unit), (raw + 5 * unit, 6 * unit), (raw + 11 * unit, 2 * unit)]
        n, w = lax.axis_index("narrow"), lax.axis_index("wide")
        place = jnp.arange(owners, dtype=jnp.int32) ^ (w & (owners - 1))
        place = sum((((place >> b) & 1) << (low - 1 - b) for b in range(low)), jnp.zeros((owners,), jnp.int32))
        top = w >> low
        excited = excited.reshape(1, depth)
        remote = range(1, narrow)
        swap = {source: [(a, a ^ source) for a in range(narrow)] for source in remote}

        def kick_at(*args, **more):
            return kick(owners, each, groups, unit, *args, **more)

        def multiply_at(which, start, pieces, total, split=False):
            return multiply(owners, which, unit, start, place, pieces, u_real, u_imag, total, split)

        def rows_to(source, value):
            return lax.ppermute(value, "narrow", swap[source])

        head_real, head_imag = psi_real[:raw], psi_imag[:raw]
        heads = {s: (rows_to(s, head_real), rows_to(s, head_imag)) for s in remote}
        angles = {s: rows_to(s, kick_angle) for s in remote}

        table = table_of(kick_angle)
        mine = [kick_at(start, length, table, excited, psi_real, psi_imag) for start, length in cuts]
        arrived = {
            (s, g, c): rows_to(s, mine[c][g])
            for s in remote
            for g in range(len(groups))
            for c in range(len(cuts))
        }

        (tail,) = kick_at(last, unit, table, excited, psi_real, psi_imag, place=place)
        tail = tail[None]
        for b in range(low):
            half = tail.shape[1] // 2
            got = across(tail[:, half:], 1 << b)
            tail = jnp.concatenate([tail[:, :half], got], axis=0)
        u_pieces = {0: jnp.concatenate([u_real[:, last:], u_imag[:, last:]], axis=0)}
        for b in reversed(range(low)):
            for j in list(u_pieces):
                u_pieces[j | (1 << b)] = across(u_pieces[j], 1 << b)
        splits = [range(owners // 2, owners), range(0, owners // 2)]
        tails = {
            (s, i): rows_to(s, tail[js.start : js.stop : js.step].reshape(len(js) * 2 * each, unit))
            for s in remote
            for i, js in enumerate(splits)
        }

        spare = [
            (start, kick_at(start, length, table, excited, psi_real, psi_imag))
            for start, length in [(0, raw), (last, unit)]
        ]
        total = None
        for i, (start, pieces) in enumerate([(start, mine[c]) for c, (start, _) in enumerate(cuts)] + spare):
            total = multiply_at(counts, start, pieces, total, i == len(cuts) + 1)
        terms = [(0, 0, value) for value in scatter_high(scatter_low(total), 0)]

        for s in remote:
            head = kick_at(0, raw, table_of(angles[s]), excited, *heads[s], skip=False)
            values = []
            for g, count in enumerate(counts):
                total = multiply_at([count], 0, [head[g]], None)
                for c, (start, _) in enumerate(cuts):
                    split = c == len(cuts) - 1
                    total = multiply_at([count], start, [arrived[s, g, c]], total, split)
                values.append(scatter_low(total))
            if len(counts) > 1:
                terms += [(s, 0, value) for value in scatter_high(values[0], s)]
            total = None
            for i, js in enumerate(splits):
                held = [values[-1]] if i == len(splits) - 1 else []
                total = finish(each, tails[s, i], [u_pieces[j] for j in js], total, held)
            terms += [(s, 0, value) for value in scatter_high(total, s, jnp.bfloat16)]
        flags = (top == (n ^ jnp.arange(narrow, dtype=jnp.int32))).astype(jnp.int32)
        return combine(flags, terms, each, local_rows)

    in_specs = (
        P("narrow", "wide"),
        P("narrow", "wide"),
        P("wide", "narrow"),
        P("wide", "narrow"),
        P("narrow"),
        P("wide"),
    )
    out_specs = (P("wide", "narrow"), P("wide", "narrow"))
    return jax.shard_map(on_device, mesh=mesh, in_specs=in_specs, out_specs=out_specs, check_vma=False)
```
